32 devices in a mesh: band: 8 (over z, y), rep: 4 (over x, core).
Axes of the slice: x: 2, y: 2, z: 4, core: 2. Of those that a mesh axis runs over, the one named last changes fastest.
Arguments:
- embeddings: bfloat16 [128, 4096], P('rep', 'band'), may hold values from -6 to 6
- route: int32 [4096, 1], P('band'), may hold values from 0 to 7; in each aligned block of 512 rows (0 to 511, 512 to 1023, ...) at most 160 rows name the same one
- place: bfloat16 [2, 4096], P(None, 'band'), may hold values from 0 to 1
- scales: float32 [4], replicated, may hold values from 0.25 to 1
- first_weight: bfloat16 [512, 512], replicated, may hold values from -0.25 to 0.25
- first_bias: float32 [512], replicated, may hold values from -3 to 3
- second_weight: bfloat16 [512, 512], replicated, may hold values from -0.25 to 0.25
- out_cotangent: bfloat16 [512, 96, 256], P(None, ('band', 'rep')), may hold values from -6 to 6
Outputs:
- embed_gradient: float32 [128, 4096], P('rep', 'band')
- first_weight_gradient: float32 [512, 512], replicated
- first_bias_gradient: float32 [512], replicated
- second_weight_gradient: float32 [512, 512], replicated
The draws below stay inside these ranges and needn't reach their ends.
Inputs may be any that keep to these rules, and one draw needn't show every extreme that they name: `route`: within the 512 reports of one feed (aligned blocks of rows), at most 160 name the same band, and in some block exactly 160 do.
All inputs are finite; a program needn't handle non-finite values.
Results may differ from the reference program's by a relative error of at most 0.0063.
Values may be sent and summed in bfloat16 or wider, within the bound.
No kernel may reach another device: no remote copies, remote signals or barrier semaphores. Data moves between devices by JAX's collectives and lax.ppermute only.
A program may use at most 128 MiB of HBM per device.

```python
import math
import jax
import jax.numpy as jnp
import numpy as np
from jax import lax

C = 128
L = 4
HID = 512
OUTC = 512
LAT_DEV = 12
NLON = 256
R_DEV = 512
F = 512
CAP = 160
REPORTS = 4096
NLAT = 96
N_BAND = 8


def block_scale(rng, dims, shards, low, largest):
    def one(dim, shards_of):
        draws = jax.random.uniform(jax.random.fold_in(jax.random.fold_in(rng, 6), dim), (shards_of,), jnp.float32, low / len(shards), largest / len(shards))
        return jnp.repeat(jnp.exp(draws), dims[dim] // shards_of).reshape((-1,) + (1,) * (len(dims) - dim - 1))

    gain = one(*shards[0])
    for cut in shards[1:]:
        gain = gain * one(*cut)
    return gain


def deal_out(stream_key, own, number, rows, count, top, limit, slope):
    ranking = jax.random.permutation(stream_key, count)
    crowded, ordinary = shares(count, rows * top, limit, slope, True), shares(count, rows * top, limit, slope, False)
    places = jnp.arange(count)

    def named(lengths, offset_by):
        used = int((lengths > 0).sum())
        fixed = max(1, used // 4)
        shifted = fixed + (places - fixed + offset_by * (used - fixed)) % max(1, count - fixed)
        return jnp.zeros((count,), jnp.int32).at[ranking[jnp.where(places < fixed, places, shifted)]].set(jnp.asarray(lengths, jnp.int32))

    lengths = jnp.where(number % 4 == 0, named(crowded, number // 4), named(ordinary, number - number // 4 - 1))
    mixed = jax.random.permutation(jax.random.fold_in(own, 3), count)
    donor, taker = mixed[0:count // 2 * 2:2], mixed[1:count // 2 * 2:2]
    margin = jnp.minimum(lengths[donor] - 1, limit - lengths[taker]) // 2
    margin = jnp.where((donor == ranking[0]) | (taker == ranking[0]) | (lengths[taker] == 0), 0, jnp.maximum(margin, 0))
    shifted = jax.random.randint(jax.random.fold_in(own, 4), (count // 2,), 0, 1 << 20) % (margin + 1)
    lengths = lengths.at[donor].add(-shifted).at[taker].add(shifted)
    items = jnp.searchsorted(jnp.cumsum(lengths), jnp.arange(rows * top), side="right").astype(jnp.int32)
    listing = items.reshape(top, rows).T
    listing = listing[jax.random.permutation(jax.random.fold_in(own, 1), rows)]
    offset_by = jax.random.randint(jax.random.fold_in(own, 2), (rows, 1), 0, top)
    return jnp.take_along_axis(listing, (jnp.arange(top)[None, :] + offset_by) % top, axis=1)


def shares(number_of, total, most, lean, full):
    portions = [(1 << 20) // math.isqrt(rank ** lean) + 1 for rank in range(1, number_of + 1)]
    largest = most if full else min(most, max(-(-total // number_of), total * portions[0] // sum(portions)))
    least = 1 if total - largest >= number_of - 1 else 0
    given, surplus = [largest] + [least] * (number_of - 1), total - largest - least * (number_of - 1)
    while surplus > 0:
        movable = [i for i in range(1, number_of) if given[i] < largest] or [i for i in range(1, number_of) if given[i] < most]
        pool, remaining = sum([portions[i] for i in movable]), surplus
        for i in movable:
            extra = min(most - given[i], max(1, remaining * portions[i] // pool), surplus)
            given[i] = given[i] + extra
            surplus = surplus - extra
    return np.array(given)


def gaussian(rng, extent, deviation, bound, cuts=(), kind=jnp.bfloat16):
    drawn = deviation * jax.random.normal(rng, extent, jnp.float32)
    if cuts:
        drawn = drawn * block_scale(rng, extent, cuts, -0.22, 0.18)
    return jnp.clip(drawn, -bound, bound).astype(kind)


def setup_inputs(seed: int = 0) -> dict:
    streams_of = jax.random.split(jax.random.key(seed), 9)
    embeddings = gaussian(streams_of[0], (C, REPORTS), 1.0, 6.0, ((0, 4), (1, 8)))
    route_keys = jax.random.split(jax.random.fold_in(streams_of[1], 1), REPORTS // R_DEV)
    route_turns = jax.random.permutation(jax.random.fold_in(streams_of[1], 3), REPORTS // R_DEV)
    route = jax.vmap(lambda own, number: deal_out(jax.random.fold_in(streams_of[1], 2), own, number, R_DEV, N_BAND, 1, CAP, 2))(route_keys, route_turns).reshape((REPORTS, 1))
    place = jnp.clip(1.0 * jax.random.uniform(streams_of[2], (2, REPORTS), jnp.float32) ** block_scale(streams_of[2], (2, REPORTS), ((1, 8),), -0.2, 0.2), 0.0, 1.0).astype(jnp.bfloat16)
    scales = jnp.clip(jnp.exp(jax.random.uniform(streams_of[3], (L,), jnp.float32, math.log(0.25), math.log(1.0))), 0.25, 1.0)
    first_weight = gaussian(streams_of[4], (F, HID), F ** -0.5, 0.25)
    first_bias = gaussian(streams_of[5], (HID,), 0.5, 3.0, (), jnp.float32)
    second_weight = gaussian(streams_of[6], (HID, OUTC), HID ** -0.5, 0.25)
    out_cotangent = gaussian(streams_of[7], (OUTC, NLAT, NLON), 1.0, 6.0, ((1, 32),))
    return {"embeddings": embeddings, "route": route, "place": place, "scales": scales, "first_weight": first_weight, "first_bias": first_bias, "second_weight": second_weight, "out_cotangent": out_cotangent}


root_two_pi = 0.7978845608028654
cubic = 0.044715


def gelu_value(value):
    inner = root_two_pi * (value + cubic * value * value * value)
    return 0.5 * value * (1.0 + jnp.tanh(inner))


def gelu_slope(value):
    tangent = jnp.tanh(root_two_pi * (value + cubic * value * value * value))
    return 0.5 * (1.0 + tangent) + 0.5 * value * (1.0 - tangent * tangent) * root_two_pi * (1.0 + 3.0 * cubic * value * value)


def kernel_factors(geometry, block, scales, lat_rows, columns):
    north_fraction = geometry[0]
    east_fraction = geometry[1]
    valid = geometry[2]
    centre_rows = jnp.arange(lat_rows, dtype=jnp.float32) + 0.5
    north_gap = ((1 - block).astype(jnp.float32) * lat_rows)[None, :] + centre_rows[:, None] - (north_fraction * lat_rows)[None, :]
    east_gap = (jnp.arange(columns, dtype=jnp.float32) + 0.5)[:, None] - (east_fraction * columns)[None, :]
    reach = scales * lat_rows
    inverse = 0.5 / (reach * reach)
    row_kernel = (jnp.exp(-(north_gap * north_gap)[None] * inverse[:, None, None]) * valid[None, None, :]).astype(jnp.bfloat16)
    column_kernel = jnp.exp(-(east_gap * east_gap)[None] * inverse[:, None, None]).astype(jnp.bfloat16)
    return row_kernel, column_kernel


def splat(embedded, row_kernel, column_kernel):
    channels = embedded.shape[0]
    levels, lat_rows, slots = row_kernel.shape
    columns = column_kernel.shape[1]
    sums = []
    weights = []
    for level in range(levels):
        weighted = (embedded[:, None, :] * row_kernel[level][None]).reshape(channels * lat_rows, slots)
        sums.append(lax.dot_general(weighted, column_kernel[level], (((1,), (1,)), ((), ())), preferred_element_type=jnp.float32))
        weights.append(lax.dot_general(row_kernel[level], column_kernel[level], (((1,), (1,)), ((), ())), preferred_element_type=jnp.float32))
    splatted = jnp.stack(sums).reshape(levels, channels, lat_rows * columns)
    density = jnp.stack(weights).reshape(levels, lat_rows * columns)
    features = (splatted / (density[:, None, :] + 1.0)).transpose(1, 0, 2).reshape(channels * levels, lat_rows * columns).astype(jnp.bfloat16)
    return features, density


def spread_back(gradient, row_kernel, column_kernel):
    levels, lat_rows, slots = row_kernel.shape
    columns = column_kernel.shape[1]
    channels = gradient.shape[0] // levels
    grid = gradient.reshape(channels, levels, lat_rows * columns)
    total = jnp.zeros((channels, slots), jnp.float32)
    for level in range(levels):
        slab = grid[:, level].reshape(channels * lat_rows, columns)
        along = jnp.dot(slab, column_kernel[level], preferred_element_type=jnp.float32).reshape(channels, lat_rows, slots)
        total = total + jnp.sum(along * row_kernel[level][None].astype(jnp.float32), axis=1)
    return total


def reference(embeddings, route, place, scales, first_weight, first_bias, second_weight, out_cotangent):
    channels, total = embeddings.shape
    bands = N_BAND
    capacity = CAP
    reports = R_DEV
    lat_rows = LAT_DEV
    columns = NLON
    levels = L
    cells = lat_rows * columns
    slots = bands * capacity
    owner = route[:, 0].reshape(bands, reports)
    onehot = (owner[:, :, None] == jnp.arange(bands, dtype=jnp.int32)[None, None, :]).astype(jnp.int32)
    running = jnp.cumsum(onehot, axis=1)
    rank = jnp.sum((running - 1) * onehot, axis=2)
    source = jnp.arange(bands, dtype=jnp.int32)[:, None] * jnp.ones((1, reports), jnp.int32)
    position = (owner * slots + source * capacity + rank).reshape(-1).astype(jnp.int32)
    table = jnp.full((bands * slots,), -1, jnp.int32).at[position].set(jnp.arange(total, dtype=jnp.int32))
    table = table.reshape(bands, slots)
    empty = jnp.full((1, slots), -1, jnp.int32)
    padded = jnp.concatenate([empty, table, empty], axis=0)
    block = (jnp.arange(3 * slots, dtype=jnp.int32) // slots).astype(jnp.int32)
    packed_all = jnp.concatenate([embeddings, place, jnp.ones((1, total), jnp.bfloat16)], axis=0)

    def one_band(carry, band):
        gradient_sum, first_sum, bias_sum, second_sum = carry
        members = lax.dynamic_slice_in_dim(padded, band, 3, 0).reshape(-1)
        valid = members >= 0
        safe = jnp.where(valid, members, 0).astype(jnp.int32)
        gathered = jnp.where(valid[None, :], packed_all[:, safe], jnp.zeros((), jnp.bfloat16))
        embedded = gathered[:channels]
        geometry = gathered[channels:].astype(jnp.float32)
        row_kernel, column_kernel = kernel_factors(geometry, block, scales, lat_rows, columns)
        features, density = splat(embedded, row_kernel, column_kernel)
        cotangent = lax.dynamic_slice_in_dim(out_cotangent, (band * lat_rows).astype(jnp.int32), lat_rows, 1).reshape(out_cotangent.shape[0], cells)
        preact = lax.dot_general(first_weight, features, (((0,), (0,)), ((), ())), preferred_element_type=jnp.float32) + first_bias[:, None]
        hidden = gelu_value(preact).astype(jnp.bfloat16)
        pre_gradient = (jnp.dot(second_weight, cotangent, preferred_element_type=jnp.float32) * gelu_slope(preact)).astype(jnp.bfloat16)
        first_sum = first_sum + lax.dot_general(features, pre_gradient, (((1,), (1,)), ((), ())), preferred_element_type=jnp.float32)
        second_sum = second_sum + lax.dot_general(hidden, cotangent, (((1,), (1,)), ((), ())), preferred_element_type=jnp.float32)
        bias_sum = bias_sum + jnp.sum(pre_gradient.astype(jnp.float32), axis=1)
        feature_gradient = jnp.dot(first_weight, pre_gradient, preferred_element_type=jnp.float32)
        splat_gradient = (feature_gradient.reshape(channels, levels, cells) / (density[None] + 1.0)).reshape(channels * levels, cells).astype(jnp.bfloat16)
        slot_gradient = spread_back(splat_gradient, row_kernel, column_kernel)
        gradient_sum = gradient_sum.at[:, safe].add(jnp.where(valid[None, :], slot_gradient, 0.0))
        return (gradient_sum, first_sum, bias_sum, second_sum), None

    start = (jnp.zeros((channels, total), jnp.float32),
             jnp.zeros(first_weight.shape, jnp.float32),
             jnp.zeros(first_bias.shape, jnp.float32),
             jnp.zeros(second_weight.shape, jnp.float32))
    final, _ = lax.scan(one_band, start, jnp.arange(bands, dtype=jnp.int32))
    return final[0], final[1], final[2], final[3]
```

```python
import jax
import jax.numpy as jnp
from jax import lax
from jax.experimental import pallas as pl
from jax.experimental.pallas import tpu as pltpu
from jax.sharding import PartitionSpec as P

root_two_pi = 0.7978845608028654
cubic = 0.044715


def padded(cells, sides, width):
    for axis, dim in sides:
        count = lax.axis_size(axis)
        ends = count - 1
        head = lax.slice_in_dim(cells, 0, width, axis=dim)
        tail = lax.slice_in_dim(cells, cells.shape[dim] - width, cells.shape[dim], axis=dim)
        cells = jnp.concatenate(
            [
                lax.ppermute(tail, axis, [(i, (i + 1) % count) for i in range(ends)]),
                cells,
                lax.ppermute(head, axis, [((i + 1) % count, i) for i in range(ends)]),
            ],
            axis=dim,
        )
    return cells


def gelu_value(value):
    inner = root_two_pi * (value + cubic * value * value * value)
    return 0.5 * value * (1.0 + jnp.tanh(inner))


def gelu_slope(value):
    tangent = jnp.tanh(root_two_pi * (value + cubic * value * value * value))
    return 0.5 * (1.0 + tangent) + 0.5 * value * (1.0 - tangent * tangent) * root_two_pi * (
        1.0 + 3.0 * cubic * value * value
    )


def kernel_factors(geometry, block, scales, lat_rows, columns):
    north_fraction = geometry[0]
    east_fraction = geometry[1]
    valid = geometry[2]
    centre_rows = jnp.arange(lat_rows, dtype=jnp.float32) + 0.5
    north_gap = (
        ((1 - block).astype(jnp.float32) * lat_rows)[None, :]
        + centre_rows[:, None]
        - (north_fraction * lat_rows)[None, :]
    )
    east_gap = (jnp.arange(columns, dtype=jnp.float32) + 0.5)[:, None] - (east_fraction * columns)[
        None, :
    ]
    reach = scales * lat_rows
    inverse = 0.5 / (reach * reach)
    row_kernel = (
        jnp.exp(-(north_gap * north_gap)[None] * inverse[:, None, None]) * valid[None, None, :]
    ).astype(jnp.bfloat16)
    column_kernel = jnp.exp(-(east_gap * east_gap)[None] * inverse[:, None, None]).astype(
        jnp.bfloat16
    )
    return (row_kernel, column_kernel)


def splat(embedded, row_kernel, column_kernel):
    channels = embedded.shape[0]
    levels, lat_rows, slots = row_kernel.shape
    columns = column_kernel.shape[1]
    sums = []
    weights = []
    for level in range(levels):
        weighted = (embedded[:, None, :] * row_kernel[level][None]).reshape(
            channels * lat_rows, slots
        )
        sums.append(
            lax.dot_general(
                weighted,
                column_kernel[level],
                (((1,), (1,)), ((), ())),
                preferred_element_type=jnp.float32,
            )
        )
        weights.append(
            lax.dot_general(
                row_kernel[level],
                column_kernel[level],
                (((1,), (1,)), ((), ())),
                preferred_element_type=jnp.float32,
            )
        )
    splatted = jnp.stack(sums).reshape(levels, channels, lat_rows * columns)
    density = jnp.stack(weights).reshape(levels, lat_rows * columns)
    features = (
        (splatted / (density[:, None, :] + 1.0))
        .transpose(1, 0, 2)
        .reshape(channels * levels, lat_rows * columns)
        .astype(jnp.bfloat16)
    )
    return (features, density)


def spread_back(gradient, row_kernel, column_kernel):
    levels, lat_rows, slots = row_kernel.shape
    columns = column_kernel.shape[1]
    channels = gradient.shape[0] // levels
    grid = gradient.reshape(channels, levels, lat_rows * columns)
    total = jnp.zeros((channels, slots), jnp.float32)
    for level in range(levels):
        slab = grid[:, level].reshape(channels * lat_rows, columns)
        along = jnp.dot(slab, column_kernel[level], preferred_element_type=jnp.float32).reshape(
            channels, lat_rows, slots
        )
        total = total + jnp.sum(along * row_kernel[level][None].astype(jnp.float32), axis=1)
    return total


def band_ranks(route_rows, bands):
    owner = route_rows[:, 0]
    onehot = (owner[:, None] == jnp.arange(bands, dtype=jnp.int32)[None, :]).astype(jnp.int32)
    running = jnp.cumsum(onehot, axis=0)
    return (owner, jnp.sum((running - 1) * onehot, axis=1))


def routed(
    embeddings, route, place, scales, first_weight, first_bias, second_weight, out_cotangent
):
    channels, reports = embeddings.shape
    bands = lax.axis_size("band")
    parts = lax.axis_size("rep")
    quarter = lax.axis_index("rep")
    capacity = max(2, 5 * reports // (2 * bands))
    sub_rows = out_cotangent.shape[1]
    lat_rows = sub_rows * parts
    columns = out_cotangent.shape[2]
    levels = scales.shape[0]
    owner, rank = band_ranks(route, bands)
    packed = jnp.concatenate([embeddings, place, jnp.ones((1, reports), jnp.bfloat16)], axis=0)
    rows = channels + 3
    whole = bands * capacity
    outgoing = jnp.zeros((rows, whole), jnp.bfloat16).at[:, owner * capacity + rank].set(packed)
    arrived = lax.all_to_all(outgoing, "band", split_axis=1, concat_axis=1, tiled=True)
    nearby = padded(arrived, (("band", 1),), whole)
    block = jnp.arange(3 * whole, dtype=jnp.int32) // whole
    geometry = nearby[channels:].astype(jnp.float32)
    row_kernel, column_kernel = kernel_factors(geometry, block, scales, lat_rows, columns)
    features, density = splat(nearby[:channels], row_kernel, column_kernel)
    cotangent = out_cotangent.reshape(out_cotangent.shape[0], sub_rows * columns)
    mine = lax.all_to_all(features, "rep", split_axis=1, concat_axis=0, tiled=True)
    local_density = lax.dynamic_slice_in_dim(
        density.reshape(levels, lat_rows, columns), quarter * sub_rows, sub_rows, 1
    ).reshape(levels, sub_rows * columns)
    preact = (
        lax.dot_general(
            first_weight, mine, (((0,), (0,)), ((), ())), preferred_element_type=jnp.float32
        )
        + first_bias[:, None]
    )
    hidden = gelu_value(preact).astype(jnp.bfloat16)
    pre_gradient = (
        jnp.dot(second_weight, cotangent, preferred_element_type=jnp.float32) * gelu_slope(preact)
    ).astype(jnp.bfloat16)
    first_sum = lax.dot_general(
        mine, pre_gradient, (((1,), (1,)), ((), ())), preferred_element_type=jnp.float32
    )
    second_sum = lax.dot_general(
        hidden, cotangent, (((1,), (1,)), ((), ())), preferred_element_type=jnp.float32
    )
    bias_sum = jnp.sum(pre_gradient.astype(jnp.float32), axis=1)
    feature_gradient = jnp.dot(first_weight, pre_gradient, preferred_element_type=jnp.float32)
    count = sub_rows * columns
    cell_part = (
        (feature_gradient.reshape(-1, levels, count) / (local_density[None] + 1.0))
        .reshape(-1, count)
        .astype(jnp.bfloat16)
    )
    splat_gradient = lax.all_to_all(cell_part, "rep", split_axis=0, concat_axis=1, tiled=True)
    totals = lax.psum((first_sum, second_sum, bias_sum), ("band", "rep"))
    slot_gradient = spread_back(splat_gradient, row_kernel, column_kernel)
    outward = jnp.concatenate([slot_gradient[:, :whole], slot_gradient[:, 2 * whole :]], axis=1)
    returned = padded(outward, (("band", 1),), whole)
    own_total = slot_gradient[:, whole : 2 * whole] + returned[:, :whole] + returned[:, 3 * whole :]
    backward = lax.all_to_all(own_total, "band", split_axis=1, concat_axis=1, tiled=True)
    embed_gradient = backward[:, owner * capacity + rank]
    return (embed_gradient, totals[0], totals[2], totals[1])


AXES = ("band", "rep")
BF16 = jnp.bfloat16
F32 = jnp.float32
NT = (((1,), (1,)), ((), ()))
ROW_TILE = 16
LANES = 128


def vmem(mib):
    return pltpu.CompilerParams(vmem_limit_bytes=mib * 1024 * 1024)


class Layout:
    def __init__(self, bands, parts):
        self.bands, self.parts = bands, parts
        self.half = parts // 2
        self.core = list(range(self.half))
        self.near = [0, parts, self.half, parts + self.half]
        self.far = [2 * parts * k for k in range(bands // 2)]
        self.masks = [c ^ n ^ f for c in self.core for n in self.near for f in self.far]

    def swap(self, value, mask):
        count = self.bands * self.parts
        return lax.ppermute(value, AXES, [(i, i ^ mask) for i in range(count)])

    def gather(self, value):
        far = jnp.stack([value] + [self.swap(value, mask) for mask in self.far[1:]])
        near = jnp.concatenate([far] + [self.swap(far, mask) for mask in self.near[1:]])
        return [near] + [self.swap(near, mask) for mask in self.core[1:]]

    def scatter(self, pieces):
        total = pieces[0].astype(F32)
        for mask, piece in zip(self.core[1:], pieces[1:]):
            total = total + self.swap(piece, mask).astype(F32)
        for group in (self.near, self.far):
            total = total.reshape((len(group), -1) + total.shape[1:])
            sent = total[1:].astype(BF16)
            total = total[0]
            for index, mask in enumerate(group[1:]):
                total = total + self.swap(sent[index], mask).astype(F32)
        return total[0]


def pack_kernel(emb_ref, place_ref, owner_ref, out_ref):
    channels, reports = emb_ref.shape
    out_ref[:, :reports] = emb_ref[...]
    rows = [place_ref[0:1, :].astype(F32), place_ref[1:2, :].astype(F32), owner_ref[...].astype(F32)]
    spans = reports // LANES
    parts = [row[:, k * LANES : (k + 1) * LANES] for row in rows for k in range(spans)]
    parts.append(jnp.zeros((channels - 3 * spans, LANES), F32))
    out_ref[:, reports:] = jnp.concatenate(parts, axis=0).astype(BF16)


def geometry_row(table, first, spans):
    return jnp.concatenate([table[first + k : first + k + 1, :] for k in range(spans)], axis=1)


def factor_kernel(sub_rows, parts, scales_ref, own_ref, other_ref, col_ref, row_ref):
    step = pl.program_id(0)
    groups = own_ref.shape[0]
    levels, columns, reports = col_ref.shape
    lat_rows = sub_rows * parts
    spans = reports // LANES
    band = lax.axis_index("band")
    quarter = lax.axis_index("rep")
    far = lax.rem(step, groups)
    table = jnp.where(step < groups, own_ref[far].astype(F32), other_ref[far].astype(F32))
    north = geometry_row(table, 0, spans)
    east = geometry_row(table, spans, spans)
    owner = geometry_row(table, 2 * spans, spans)
    inverse = []
    for level in range(levels):
        reach = scales_ref[level] * lat_rows
        inverse.append(0.5 / (reach * reach))
    centre = lax.broadcasted_iota(jnp.int32, (columns, reports), 0).astype(F32) + 0.5
    east_gap = centre - east * columns
    east_square = -(east_gap * east_gap)
    for level in range(levels):
        col_ref[level] = jnp.exp(east_square * inverse[level]).astype(BF16)
    rows = row_ref.shape[0]
    index = lax.broadcasted_iota(jnp.int32, (rows, reports), 0)
    level_of = index // sub_rows
    row_of = (index - level_of * sub_rows + quarter * sub_rows).astype(F32)
    scale = jnp.zeros((rows, reports), F32)
    for level in range(levels):
        scale = jnp.where(level_of == level, inverse[level], scale)
    apart = band.astype(F32) - owner
    north_gap = apart * lat_rows + (row_of + 0.5) - north * lat_rows
    kernel = jnp.exp(-(north_gap * north_gap) * scale)
    keep = jnp.where(jnp.abs(apart) < 1.5, 1.0, 0.0) * jnp.where(level_of < levels, 1.0, 0.0)
    row_ref[...] = (kernel * keep).astype(BF16)


def factors(scales, own, other, sub_rows, parts, columns):
    groups, channels, width = own.shape
    reports = width - LANES
    levels = scales.shape[0]
    rows = -(-levels * sub_rows // ROW_TILE) * ROW_TILE
    table = pl.BlockSpec((groups, channels, LANES), lambda s: (0, 0, reports // LANES))
    steps = 2 * groups
    return pl.pallas_call(
        lambda *refs: factor_kernel(sub_rows, parts, *refs),
        grid=(steps,),
        in_specs=[pl.BlockSpec(memory_space=pltpu.SMEM), table, table],
        out_specs=[
            pl.BlockSpec((levels, columns, reports), lambda s: (0, 0, s)),
            pl.BlockSpec((rows, reports), lambda s: (0, s)),
        ],
        out_shape=[
            jax.ShapeDtypeStruct((levels, columns, steps * reports), BF16),
            jax.ShapeDtypeStruct((rows, steps * reports), BF16),
        ],
        compiler_params=vmem(16),
        name="factors",
    )(scales, own, other)


def dense_kernel(layout, sub_rows, levels, pieces, *refs):
    (row_ref, col_ref, w1t_ref, bias_ref, g_ref, cot_ref) = refs[pieces : pieces + 6]
    outs = refs[pieces + 6 : pieces + 6 + pieces]
    pre_ref, inv_ref, acc_ref, emb_ref, feat_ref, first_ref, second_ref, sum_ref = refs[2 * pieces + 6 :]
    step = pl.program_id(0)
    me_rep = lax.axis_index("rep")
    me = lax.axis_index("band") * layout.parts + me_rep
    half = layout.half
    reports = col_ref.shape[2]
    columns = col_ref.shape[1]
    part_channels = emb_ref.shape[1]
    channels = part_channels * layout.parts
    row_count = row_ref.shape[0]

    for core in range(half):
        for x in range(2):
            emb_ref[core * 2 + x] = refs[core][x, :, :reports]
    blocks = []
    for q in range(layout.parts):
        rel = q ^ me_rep
        blocks.append(emb_ref[lax.rem(rel, half) * 2 + rel // half])
    emb = jnp.concatenate(blocks, axis=0)
    row = row_ref[...]
    for level in range(levels):
        weighted = [emb * row[level * sub_rows + i : level * sub_rows + i + 1, :] for i in range(sub_rows)]
        product = lax.dot_general(
            jnp.concatenate(weighted + [row], axis=0), col_ref[level], NT, preferred_element_type=F32
        )

        @pl.when(step == 0)
        def _():
            acc_ref[level] = product

        @pl.when(step > 0)
        def _():
            acc_ref[level] += product

    @pl.when(step == pl.num_programs(0) - 1)
    def _():
        inv_ref[...] = jnp.zeros_like(inv_ref)
        for level in range(levels):
            for i in range(sub_rows):
                at = level * sub_rows + i
                density = acc_ref[level, sub_rows * channels + at : sub_rows * channels + at + 1, :]
                inverse = 1.0 / (density + 1.0)
                inv_ref[at : at + 1, :] = inverse
                feat_ref[level * channels : (level + 1) * channels, i * columns : (i + 1) * columns] = (
                    acc_ref[level, i * channels : (i + 1) * channels, :] * inverse
                ).astype(BF16)
        feats = feat_ref[...]
        cot = cot_ref[...]
        value = jnp.dot(w1t_ref[...], feats, preferred_element_type=F32) + bias_ref[...]
        square = value * value
        tangent = jnp.tanh(root_two_pi * (value + cubic * value * square))
        half_up = 0.5 * (1.0 + tangent)
        hidden = (value * half_up).astype(BF16)
        slope = half_up + 0.5 * value * (1.0 - tangent * tangent) * root_two_pi * (
            1.0 + 3.0 * cubic * square
        )
        pre = (g_ref[...] * slope).astype(BF16)
        pre_ref[...] = pre
        first = lax.dot_general(feats, pre, NT, preferred_element_type=F32)
        for j in range(first_ref.shape[0]):
            for level in range(levels):
                first_ref[j, pl.ds(level, channels, stride=levels), :] = first[
                    level * channels : (level + 1) * channels, j * LANES : (j + 1) * LANES
                ]
        second = lax.dot_general(hidden, cot, NT, preferred_element_type=F32)
        for j in range(second_ref.shape[0]):
            second_ref[j] = second[:, j * LANES : (j + 1) * LANES]
        ones = jnp.ones((ROW_TILE, pre.shape[1]), BF16)
        bias = lax.dot_general(ones, pre, NT, preferred_element_type=F32)[:8]
        spans = bias.shape[1] // LANES
        sum_ref[...] = jnp.zeros_like(sum_ref)
        for j in range(spans):
            sum_ref[j * 8 : (j + 1) * 8, :] = bias[:, j * LANES : (j + 1) * LANES]
        each = len(layout.near) * len(layout.far)
        count = layout.bands * layout.parts
        for k, mask in enumerate(layout.masks):
            device = me ^ mask
            out_ref = outs[k // each]
            base = 0
            for table in (first_ref, second_ref):
                size = table.shape[1] // count
                for j in range(table.shape[0]):
                    out_ref[k % each, base : base + size, :] = table[
                        j, pl.ds(pl.multiple_of(device * size, size), size), :
                    ].astype(BF16)
                    base += size
            out_ref[k % each, base : base + 8, :] = sum_ref[
                pl.ds(pl.multiple_of(device * 8, 8), 8), :
            ].astype(BF16)


def dense(layout, gathered, row, col, w1t, bias, g, cot, sub_rows):
    pieces = len(gathered)
    nf = len(layout.far)
    levels, columns, total = col.shape
    part_channels, width = gathered[0].shape[-2:]
    reports = width - LANES
    rows = row.shape[0]
    channels = part_channels * layout.parts
    features = channels * levels
    hid, cells = g.shape
    outc = cot.shape[0]
    each = len(layout.near) * nf
    count = layout.bands * layout.parts
    size = features // count * (hid // LANES) + hid // count * (outc // LANES) + 8
    split = [value.reshape(2, 2, nf, part_channels, width) for value in gathered]
    whole = lambda shape: pl.BlockSpec(shape, lambda s: (0,) * len(shape), pipeline_mode=pl.Buffered(1))
    return pl.pallas_call(
        lambda *refs: dense_kernel(layout, sub_rows, levels, pieces, *refs),
        grid=(2 * nf,),
        in_specs=[
            pl.BlockSpec(
                (2, None, None, part_channels, width), lambda s: (0, s // nf, lax.rem(s, nf), 0, 0)
            )
        ]
        * pieces
        + [
            pl.BlockSpec((rows, reports), lambda s: (0, s)),
            pl.BlockSpec((levels, columns, reports), lambda s: (0, 0, s)),
            whole(w1t.shape),
            whole(bias.shape),
            whole(g.shape),
            whole(cot.shape),
        ],
        out_specs=[whole((each, size, LANES))] * pieces + [whole((hid, cells)), whole((rows, columns))],
        out_shape=[jax.ShapeDtypeStruct((each, size, LANES), BF16)] * pieces
        + [jax.ShapeDtypeStruct((hid, cells), BF16), jax.ShapeDtypeStruct((rows, columns), F32)],
        scratch_shapes=[
            pltpu.VMEM((levels, sub_rows * channels + rows, columns), F32),
            pltpu.VMEM((layout.parts, part_channels, reports), BF16),
            pltpu.VMEM((features, cells), BF16),
            pltpu.VMEM((hid // LANES, features, LANES), F32),
            pltpu.VMEM((outc // LANES, hid, LANES), F32),
            pltpu.VMEM((count * 8, LANES), F32),
        ],
        compiler_params=vmem(40),
        name="dense",
    )(*split, row, col, w1t, bias, g, cot)


def spread_kernel(layout, sub_rows, levels, pieces, *refs):
    w1_ref, pre_ref, inv_ref, row_ref, col_ref = refs[:5]
    outs = refs[5 : 5 + pieces]
    grad_ref, total_ref = refs[5 + pieces :]
    step = pl.program_id(0)
    me_rep = lax.axis_index("rep")
    columns = col_ref.shape[1]
    channels = grad_ref.shape[1] // sub_rows
    part_channels = channels // layout.parts

    @pl.when(step == 0)
    def _():
        grad = jnp.dot(w1_ref[...], pre_ref[...], preferred_element_type=F32)
        for level in range(levels):
            for i in range(sub_rows):
                at = level * sub_rows + i
                grad_ref[level, i * channels : (i + 1) * channels, :] = (
                    grad[level * channels : (level + 1) * channels, i * columns : (i + 1) * columns]
                    * inv_ref[at : at + 1, :]
                ).astype(BF16)

    total = None
    for level in range(levels):
        along = jnp.dot(grad_ref[level], col_ref[level], preferred_element_type=F32)
        for i in range(sub_rows):
            at = level * sub_rows + i
            term = along[i * channels : (i + 1) * channels, :] * row_ref[at : at + 1, :].astype(F32)
            total = term if total is None else total + term
    total_ref[...] = total
    for core in range(pieces):
        for x in range(2):
            q = (x * layout.half + core) ^ me_rep
            outs[core][x] = total_ref[
                pl.ds(pl.multiple_of(q * part_channels, part_channels), part_channels), :
            ].astype(BF16)


def spread(layout, w1, pre, inv, row, col, sub_rows):
    pieces = layout.half
    nf = len(layout.far)
    levels, columns, total = col.shape
    reports = total // (2 * nf)
    rows = row.shape[0]
    channels = w1.shape[0] // levels
    part_channels = channels // layout.parts
    whole = lambda shape: pl.BlockSpec(shape, lambda s: (0,) * len(shape), pipeline_mode=pl.Buffered(1))
    out = pl.pallas_call(
        lambda *refs: spread_kernel(layout, sub_rows, levels, pieces, *refs),
        grid=(2 * nf,),
        in_specs=[
            whole(w1.shape),
            whole(pre.shape),
            whole(inv.shape),
            pl.BlockSpec((rows, reports), lambda s: (0, s)),
            pl.BlockSpec((levels, columns, reports), lambda s: (0, 0, s)),
        ],
        out_specs=[
            pl.BlockSpec(
                (2, None, None, part_channels, reports), lambda s: (0, s // nf, lax.rem(s, nf), 0, 0)
            )
        ]
        * pieces,
        out_shape=[jax.ShapeDtypeStruct((2, 2, nf, part_channels, reports), BF16)] * pieces,
        scratch_shapes=[
            pltpu.VMEM((levels, sub_rows * channels, columns), BF16),
            pltpu.VMEM((channels, reports), F32),
        ],
        compiler_params=vmem(24),
        name="spread",
    )(w1, pre, inv, row, col)
    return [value.reshape(4 * nf, part_channels, reports) for value in out]


def unpack_kernel(layout, pieces, *refs):
    first_ref, bias_ref, second_ref, sum_ref = refs[pieces:]
    me = lax.axis_index("band") * layout.parts + lax.axis_index("rep")
    each = refs[0].shape[0]
    count = layout.bands * layout.parts
    for k, mask in enumerate(layout.masks):
        device = me ^ mask
        source = refs[k // each]
        base = 0
        for table in (first_ref, second_ref):
            size = table.shape[0] // count
            at = pl.ds(pl.multiple_of(device * size, size), size)
            for j in range(table.shape[1] // LANES):
                table[at, j * LANES : (j + 1) * LANES] = source[k % each, base : base + size, :].astype(F32)
                base += size
        sum_ref[pl.ds(pl.multiple_of(device * 8, 8), 8), :] = source[k % each, base : base + 8, :].astype(F32)
    for j in range(bias_ref.shape[1] // LANES):
        bias_ref[:, j * LANES : (j + 1) * LANES] = sum_ref[j * 8 : j * 8 + 1, :]


def unpack(layout, gathered, features, hid, outc):
    pieces = len(gathered)
    count = layout.bands * layout.parts
    return pl.pallas_call(
        lambda *refs: unpack_kernel(layout, pieces, *refs),
        out_shape=[
            jax.ShapeDtypeStruct((features, hid), F32),
            jax.ShapeDtypeStruct((1, hid), F32),
            jax.ShapeDtypeStruct((hid, outc), F32),
        ],
        scratch_shapes=[pltpu.VMEM((count * 8, LANES), F32)],
        compiler_params=vmem(16),
        name="unpack",
    )(*gathered)


def gathered_whole(
    embeddings, route, place, scales, first_weight, first_bias, second_weight, out_cotangent
):
    layout = Layout(lax.axis_size("band"), lax.axis_size("rep"))
    levels = scales.shape[0]
    outc, sub_rows, columns = out_cotangent.shape
    part_channels, reports = embeddings.shape
    features, hid = first_weight.shape
    channels = features // levels
    cells = sub_rows * columns
    packed = pl.pallas_call(
        pack_kernel,
        out_shape=jax.ShapeDtypeStruct((part_channels, reports + LANES), BF16),
        name="pack",
    )(embeddings, place, route.reshape(1, reports))
    far = jnp.stack([packed] + [layout.swap(packed, mask) for mask in layout.far[1:]])
    near = [layout.swap(far, mask) for mask in layout.near[1:]]
    col, row = factors(scales, far, near[0], sub_rows, layout.parts, columns)
    near = jnp.concatenate([far] + near)
    gathered = [near] + [layout.swap(near, mask) for mask in layout.core[1:]]

    cot = out_cotangent.reshape(outc, cells)
    w1 = first_weight.reshape(channels, levels, hid).transpose(1, 0, 2).reshape(features, hid)
    g = jnp.dot(second_weight, cot, preferred_element_type=F32)
    out = dense(layout, gathered, row, col, w1.T, first_bias[:, None], g, cot, sub_rows)
    weight_pieces, pre, inv = out[: layout.half], out[-2], out[-1]
    slots = spread(layout, w1, pre, inv, row, col, sub_rows)
    weight_chunk = layout.scatter(weight_pieces)
    embed_gradient = layout.scatter(slots)
    first, bias, second = unpack(layout, layout.gather(weight_chunk.astype(BF16)), features, hid, outc)
    return (embed_gradient, first, bias.reshape(hid), second)


def on_device(embeddings, route, place, scales, first_weight, first_bias, second_weight, out_cotangent):
    part_channels, reports = embeddings.shape
    bands, parts = lax.axis_size("band"), lax.axis_size("rep")
    capacity = max(2, 5 * reports // (2 * bands))
    few = bands * reports <= 4 * bands * capacity
    paired = parts == 4 and bands & (bands - 1) == 0 and bands >= 4
    form = gathered_whole if few and paired else routed
    return form(
        embeddings, route, place, scales, first_weight, first_bias, second_weight, out_cotangent
    )


def solution(mesh):
    return jax.shard_map(
        on_device,
        mesh=mesh,
        in_specs=(
            P("rep", "band"),
            P("band", None),
            P(None, "band"),
            P(),
            P(),
            P(),
            P(),
            P(None, ("band", "rep"), None),
        ),
        out_specs=(P("rep", "band"), P(), P(), P()),
        check_vma=False,
    )
```
